32 devices in a mesh: groups: 2 (over y), seq: 4 (over z), head: 2 (over x), prompt: 2 (over core).
Axes of the slice: x: 2, y: 2, z: 4, core: 2. Of those that a mesh axis runs over, the one named last changes fastest.
Arguments:
- prompt_queries: bfloat16 [4, 512, 2048], P(('groups', 'prompt'), 'seq', 'head'), parts along dimension 0, may hold values from -6 to 6
- prompt_keys: bfloat16 [4, 512, 2048], P(('groups', 'prompt'), 'seq', 'head'), parts along dimension 0, may hold values from -20 to 20
- prompt_values: bfloat16 [4, 512, 4096], P(('groups', 'prompt'), 'seq', 'head'), parts along dimension 0, may hold values from -6 to 6
- prompt_beta: float32 [4, 32, 512], P(('groups', 'prompt'), 'head', 'seq'), parts along dimension 0, may hold values from 0.005 to 0.15
- prompt_decay: float32 [4, 32, 512], P(('groups', 'prompt'), 'head', 'seq'), parts along dimension 0, may hold values from -0.7 to 0
- suffix_queries: bfloat16 [32, 256, 2048], P(('groups', 'seq', 'prompt'), None, 'head'), parts along dimension 0, may hold values from -6 to 6
- suffix_keys: bfloat16 [32, 256, 2048], P(('groups', 'seq', 'prompt'), None, 'head'), parts along dimension 0, may hold values from -20 to 20
- suffix_values: bfloat16 [32, 256, 4096], P(('groups', 'seq', 'prompt'), None, 'head'), parts along dimension 0, may hold values from -6 to 6
- suffix_beta: float32 [32, 32, 256], P(('groups', 'seq', 'prompt'), 'head'), parts along dimension 0, may hold values from 0.005 to 0.15
- suffix_decay: float32 [32, 32, 256], P(('groups', 'seq', 'prompt'), 'head'), parts along dimension 0, may hold values from -0.2 to 0
- norm_gain: float32 [128], replicated, may hold values from 0.25 to 1.75
- slot_branch: int32 [32], P('groups'), parts along dimension 0, may hold values from 0 to 15, each once
- branch_length: int32 [32], P('groups'), parts along dimension 0, may hold values from 1 to 256, 2048 in all
- branch_prompt: int32 [32], P('groups'), parts along dimension 0, may hold values from 0 to 1
Outputs:
- prompt_out: bfloat16 [4, 512, 4096], P(('groups', 'prompt'), 'seq', 'head'), parts along dimension 0
- suffix_out: bfloat16 [32, 256, 4096], P(('groups', 'seq', 'prompt'), None, 'head'), parts along dimension 0
The draws below stay inside these ranges and needn't reach their ends.
There are 2 independent parts, one for each index of `groups`. The reference program is written for one: setup_inputs(seed, part) draws one part's arguments, and reference() takes and returns one part's arrays. A program takes and returns all parts, laid end to end along the dimension named above; an argument that names none is the same for every part. Nothing has to cross between parts.
Inputs may be any that keep to these rules, and one draw needn't show every extreme that they name: slot_branch names every branch exactly once. `branch_length`: the lengths sum to 2048 and one of them is exactly 256.
All inputs are finite; a program needn't handle non-finite values.
Results may differ from the reference program's by a relative error of at most 0.0067.
Values sent between devices are 32-bit elements; how exact they have to be, the bound alone decides.
A program may use at most 128 MiB of HBM per device.

```python
import math
import jax
import jax.numpy as jnp
import numpy as np
from jax import lax

DK = 128
DV = 128
OUTPUT_HEAD_NUM = 32
HK = 16
TOK_DEV = 128
SUF = 256
QUERY_TEXT_SPAN = 512
PROMPT_COUNT = 2
BRANCHES = 16


def fast_heads(key):
    head_picks = jax.random.randint(jax.random.fold_in(key, 101), (OUTPUT_HEAD_NUM,), 0, 2)
    return head_picks == 0


def channel_scales(key):
    return jnp.exp(jax.random.uniform(jax.random.fold_in(key, 202), (HK * DK,), jnp.float32, -1.2, 1.2))


def key_draw(key, noise_generator_key, shape):
    noise_part = jnp.clip(jax.random.normal(jax.random.fold_in(key, noise_generator_key), shape, jnp.float32), -4.0, 4.0)
    return (noise_part * channel_scales(key)).astype(jnp.bfloat16)


def beta_draw(key, noise_generator_key, prefix_number, length):
    quick_channel_selector = fast_heads(key)[None, :, None]
    quick_forget_bound = jax.random.uniform(jax.random.fold_in(key, noise_generator_key), (prefix_number, OUTPUT_HEAD_NUM, 1), jnp.float32, 0.02, 0.1)
    gentle = jnp.exp(jax.random.uniform(jax.random.fold_in(key, noise_generator_key + 1), (prefix_number, OUTPUT_HEAD_NUM, 1), jnp.float32, -4.6, -3.0))
    jitter = jax.random.uniform(jax.random.fold_in(key, noise_generator_key + 2), (prefix_number, OUTPUT_HEAD_NUM, length), jnp.float32, 0.6, 1.4)
    return jnp.where(quick_channel_selector, quick_forget_bound, gentle) * jitter


def decay_draw(key, noise_generator_key, prefix_number, length, tile_extent):
    quick_channel_selector = fast_heads(key)[None, :, None]
    tile_total = length // tile_extent
    spike_span = min(32, tile_extent // 4)
    quick_forget_bound = jax.random.uniform(jax.random.fold_in(key, noise_generator_key), (prefix_number, OUTPUT_HEAD_NUM, 1), jnp.float32, 1.0 / 50.0, 1.0 / 40.0)
    spike_start_slot = jax.random.randint(jax.random.fold_in(key, noise_generator_key + 3), (prefix_number, OUTPUT_HEAD_NUM, tile_total), 0, tile_extent - spike_span + 1)
    spike_start_slot = jnp.repeat(spike_start_slot, tile_extent, axis=2)
    tile_offset = (jnp.arange(length, dtype=jnp.int32) % tile_extent)[None, None, :]
    within_spike = (tile_offset >= spike_start_slot) & (tile_offset < spike_start_slot + spike_span)
    forget_lower_bound = jnp.where(quick_channel_selector & within_spike, quick_forget_bound, 0.25 / QUERY_TEXT_SPAN)
    spread_factor = jnp.exp(jax.random.uniform(jax.random.fold_in(key, noise_generator_key + 1), (prefix_number, OUTPUT_HEAD_NUM, tile_total), jnp.float32, -0.7, 0.7))
    spread_factor = jnp.repeat(spread_factor, tile_extent, axis=2)
    jitter = jax.random.uniform(jax.random.fold_in(key, noise_generator_key + 2), (prefix_number, OUTPUT_HEAD_NUM, length), jnp.float32, 0.7, 1.3)
    return -forget_lower_bound * spread_factor * jitter


def draw_prompt_keys(key, part):
    return key_draw(key, 211, (PROMPT_COUNT, QUERY_TEXT_SPAN, HK * DK))


def draw_suffix_keys(key, part):
    return key_draw(key, 221, (BRANCHES, SUF, HK * DK))


def draw_prompt_beta(key, part):
    return beta_draw(key, 411, PROMPT_COUNT, QUERY_TEXT_SPAN)


def draw_suffix_beta(key, part):
    return beta_draw(key, 421, BRANCHES, SUF)


def draw_prompt_decay(key, part):
    smoothed_decay = decay_draw(key, 311, PROMPT_COUNT, QUERY_TEXT_SPAN, TOK_DEV)
    spike_positions = jax.random.randint(jax.random.fold_in(key, 321), (PROMPT_COUNT, OUTPUT_HEAD_NUM, 3), 0, QUERY_TEXT_SPAN)
    place_indices = jnp.arange(QUERY_TEXT_SPAN, dtype=jnp.int32)
    spike_events = jnp.any(place_indices[None, None, :, None] == spike_positions[:, :, None, :], axis=-1)
    spike_decays = jnp.log(jax.random.uniform(jax.random.fold_in(key, 322), (PROMPT_COUNT, OUTPUT_HEAD_NUM, QUERY_TEXT_SPAN), jnp.float32, 0.5, 0.8))
    return jnp.where(spike_events, spike_decays, smoothed_decay)


def draw_suffix_decay(key, part):
    return decay_draw(key, 331, BRANCHES, SUF, SUF)


def with_ends(values, own_key, least, largest):
    index_at = [jax.random.randint(jax.random.fold_in(own_key, axis), (), 0, length) for axis, length in enumerate(values.shape)]
    main_axis = values.shape.index(max(values.shape))
    neighbour = index_at[:main_axis] + [(index_at[main_axis] + 1) % values.shape[main_axis]] + index_at[main_axis + 1:]
    return values.at[tuple(index_at)].set(least).at[tuple(neighbour)].set(largest)


def level_of(stream_key, dims, shards, smallest, top_value):
    gain, own = 1.0, jax.random.fold_in(stream_key, 6)
    for dim, shards_of in shards:
        heights = jnp.exp(jax.random.uniform(jax.random.fold_in(own, dim), (shards_of,), jnp.float32, smallest / len(shards), top_value / len(shards)))
        gain = gain * jnp.repeat(heights, dims[dim] // shards_of).reshape([-1 if axis == dim else 1 for axis in range(len(dims))])
    return gain


def length_profile(count, total, bound, slope):
    weights = [(1 << 20) // math.isqrt(grade ** slope) + 1 for grade in range(2, count + 1)]
    rest, holding = total - bound - (count - 1), [1] * (count - 1)
    while rest > 0:
        candidates = [i for i in range(count - 1) if holding[i] < bound]
        whole, left = sum([weights[i] for i in candidates]), rest
        for i in candidates:
            extra = min(bound - holding[i], max(1, left * weights[i] // whole), rest)
            holding[i] = holding[i] + extra
            rest = rest - extra
    return np.array([bound] + holding)


def ragged_sizes(key, number_of, total, most, skew):
    if number_of == 2:
        one = jax.random.randint(key, (), max(1, total - most), min(most, total - 1) + 1)
        return jnp.stack([one, total - one])
    sizes = jnp.asarray(length_profile(number_of, total, most, skew), jnp.int32)
    pairs = (number_of - 1) // 2
    source_of, receiver = sizes[1:1 + 2 * pairs:2], sizes[2:2 + 2 * pairs:2]
    margin = jnp.minimum(source_of - 1, most - receiver)
    shifted = jax.random.randint(jax.random.fold_in(key, 1), (pairs,), 0, 1 << 20) % (margin + 1)
    sizes = sizes.at[1:1 + 2 * pairs:2].set(source_of - shifted).at[2:2 + 2 * pairs:2].set(receiver + shifted)
    return sizes[jax.random.permutation(jax.random.fold_in(key, 2), number_of)]


def centred(own_key, extent, width, most, cuts=(), kind=jnp.bfloat16):
    entries = width * jax.random.normal(own_key, extent, jnp.float32)
    if cuts:
        entries = entries * level_of(own_key, extent, cuts, -0.22, 0.18)
    return jnp.clip(entries, -most, most).astype(kind)


def setup_inputs(seed: int = 0, part: int = 0) -> dict:
    streams_of = jax.random.split(jax.random.key(seed), 15)
    own_keys = jax.random.split(jax.random.fold_in(streams_of[14], part), 15)
    prompt_queries = centred(own_keys[0], (PROMPT_COUNT, QUERY_TEXT_SPAN, HK * DK), 1.0, 6.0, ((0, 2), (1, 4), (2, 2)))
    prompt_keys = draw_prompt_keys(jax.random.fold_in(jax.random.fold_in(streams_of[14], part), 71), part)
    prompt_values = centred(own_keys[2], (PROMPT_COUNT, QUERY_TEXT_SPAN, OUTPUT_HEAD_NUM * DV), 1.0, 6.0, ((0, 2), (1, 4), (2, 2)))
    prompt_beta = draw_prompt_beta(jax.random.fold_in(jax.random.fold_in(streams_of[14], part), 71), part)
    prompt_decay = draw_prompt_decay(jax.random.fold_in(jax.random.fold_in(streams_of[14], part), 71), part)
    suffix_queries = centred(own_keys[5], (BRANCHES, SUF, HK * DK), 1.0, 6.0, ((0, 8), (2, 2)))
    suffix_keys = draw_suffix_keys(jax.random.fold_in(jax.random.fold_in(streams_of[14], part), 71), part)
    suffix_values = centred(own_keys[7], (BRANCHES, SUF, OUTPUT_HEAD_NUM * DV), 1.0, 6.0, ((0, 8), (2, 2)))
    suffix_beta = draw_suffix_beta(jax.random.fold_in(jax.random.fold_in(streams_of[14], part), 71), part)
    suffix_decay = draw_suffix_decay(jax.random.fold_in(jax.random.fold_in(streams_of[14], part), 71), part)
    norm_gain = jnp.clip(1.0 + 0.15 * jax.random.normal(streams_of[10], (DV,), jnp.float32), 0.25, 1.75)
    slot_branch = jax.random.permutation(own_keys[11], BRANCHES).astype(jnp.int32)
    branch_length = ragged_sizes(own_keys[12], BRANCHES, BRANCHES * SUF // 2, SUF, 2).astype(jnp.int32)
    branch_prompt = with_ends(jax.random.randint(own_keys[13], (BRANCHES,), 0, PROMPT_COUNT), jax.random.fold_in(own_keys[13], 1), 0, PROMPT_COUNT - 1).astype(jnp.int32)
    return {"prompt_queries": prompt_queries, "prompt_keys": prompt_keys, "prompt_values": prompt_values, "prompt_beta": prompt_beta, "prompt_decay": prompt_decay, "suffix_queries": suffix_queries, "suffix_keys": suffix_keys, "suffix_values": suffix_values, "suffix_beta": suffix_beta, "suffix_decay": suffix_decay, "norm_gain": norm_gain, "slot_branch": slot_branch, "branch_length": branch_length, "branch_prompt": branch_prompt}


HIGH_PRECISION = lax.Precision.HIGHEST
EPS_NORM = 1e-06

def unit_rows(vectors):
    widened = vectors.astype(jnp.float32)
    factor = lax.rsqrt(lax.optimization_barrier(jnp.sum(widened * widened, axis=-1, keepdims=True)) + EPS_NORM)
    return (widened * factor).astype(jnp.bfloat16)

def normed(raw_out, norm_gain):
    inv_rms = lax.rsqrt(lax.optimization_barrier(jnp.mean(raw_out * raw_out, axis=-1, keepdims=True)) + EPS_NORM)
    return (raw_out * inv_rms * norm_gain).astype(jnp.bfloat16)

def prepare(queries, key_rows, value_rows, beta_rows, decay_rows):
    tokens = queries.shape[0]
    query_unit = jnp.repeat(unit_rows(queries.reshape(tokens, HK, DK)), OUTPUT_HEAD_NUM // HK, axis=1)
    key_unit = jnp.repeat(unit_rows(key_rows.reshape(tokens, HK, DK)), OUTPUT_HEAD_NUM // HK, axis=1)
    return (query_unit, key_unit, value_rows.reshape(tokens, OUTPUT_HEAD_NUM, DV), beta_rows.T, decay_rows.T)

def run_chain(start_state, query_unit, key_unit, value_rows, beta_rows, decay_rows):

    def advance(present_state, inputs):
        query_current, key_now, value_now, beta_now, decay_now = inputs
        key_single = key_now.astype(jnp.float32)
        faded_state = jnp.exp(decay_now)[:, None, None] * present_state
        retrieved_value = jnp.einsum('te,tei->ti', key_single, faded_state, precision=HIGH_PRECISION)
        written = beta_now[:, None] * (value_now.astype(jnp.float32) - retrieved_value)
        present_state = faded_state + key_single[:, :, None] * written[:, None, :]
        output_rows = jnp.einsum('te,tei->ti', query_current.astype(jnp.float32), present_state, precision=HIGH_PRECISION)
        return (present_state, output_rows)
    return lax.scan(advance, start_state, (query_unit, key_unit, value_rows, beta_rows, decay_rows))

def reference(prompt_queries, prompt_keys, prompt_values, prompt_beta, prompt_decay, suffix_queries, suffix_keys, suffix_values, suffix_beta, suffix_decay, norm_gain, slot_branch, branch_length, branch_prompt):
    zero_state = jnp.zeros((OUTPUT_HEAD_NUM, DK, DV), jnp.float32)
    finals = []
    prompt_rows = []
    for prompt_index in range(PROMPT_COUNT):
        prepared = prepare(prompt_queries[prompt_index], prompt_keys[prompt_index], prompt_values[prompt_index], prompt_beta[prompt_index], prompt_decay[prompt_index])
        final_state, output_rows = run_chain(zero_state, prepared[0], prepared[1], prepared[2], prepared[3], prepared[4])
        finals.append(final_state)
        prompt_rows.append(normed(output_rows, norm_gain).reshape(QUERY_TEXT_SPAN, OUTPUT_HEAD_NUM * DV))
    prompt_out = jnp.stack(prompt_rows)
    final_states = jnp.stack(finals)
    slot_index = slot_branch.astype(jnp.int32)
    lengths = branch_length[slot_index]
    owners = branch_prompt[slot_index].astype(jnp.int32)
    seed_states = final_states[owners]

    def run_slot(seed_state, queries, key_rows, value_rows, beta_rows, decay_rows):
        prepared = prepare(queries, key_rows, value_rows, beta_rows, decay_rows)
        ignored, output_rows = run_chain(seed_state, prepared[0], prepared[1], prepared[2], prepared[3], prepared[4])
        return normed(output_rows, norm_gain)
    suffix_rows = jax.vmap(run_slot)(seed_states, suffix_queries, suffix_keys, suffix_values, suffix_beta, suffix_decay)
    live_rows = jnp.arange(SUF, dtype=jnp.int32)[None, :] < lengths[:, None]
    suffix_out = jnp.where(live_rows[:, :, None, None], suffix_rows, jnp.zeros((), jnp.bfloat16)).reshape(BRANCHES, SUF, OUTPUT_HEAD_NUM * DV)
    return (prompt_out, suffix_out)
```

```python
import functools

import jax
import jax.numpy as jnp
from jax import lax
from jax.experimental import pallas as pl
from jax.experimental.pallas import tpu as pltpu
from jax.sharding import PartitionSpec as P

DK = 128
DV = 128
CH = 128
EPS_NORM = 1e-06
F32 = jnp.float32
BF16 = jnp.bfloat16
NN = (((1,), (0,)), ((), ()))
NT = (((1,), (1,)), ((), ()))
TN = (((0,), (0,)), ((), ()))


def mm(a, b, dims=NN):
    return lax.dot_general(a, b, dims, preferred_element_type=F32)


def unit(x):
    w = x.astype(F32)
    return (w * lax.rsqrt(jnp.sum(w * w, axis=-1, keepdims=True) + EPS_NORM)).astype(BF16)


def iotas():
    return (
        lax.broadcasted_iota(jnp.int32, (CH, CH), 0),
        lax.broadcasted_iota(jnp.int32, (CH, CH), 1),
    )


def running_log(decay):
    rows, cols = iotas()
    tri = jnp.where(rows <= cols, 1.0, 0.0).astype(F32)
    return lax.dot_general(
        decay, tri, NN, precision=lax.Precision.HIGHEST, preferred_element_type=F32
    )


def pre_kernel(rep, q_ref, k_ref, beta_ref, decay_ref, qk_ref, solve_ref, gram_ref):
    key_heads = q_ref.shape[2] // DK
    heads = key_heads * rep
    rows, cols = iotas()
    upto = rows >= cols
    strict = rows > cols
    apart = rows ^ cols
    log_row = running_log(decay_ref[0])
    log_col = log_row.T
    beta_row = beta_ref[0]
    beta_col = beta_row.T
    lower = []
    for j in range(key_heads):
        q = unit(q_ref[0, :, j * DK : (j + 1) * DK])
        k = unit(k_ref[0, :, j * DK : (j + 1) * DK])
        qk_ref[0, 0, j, :CH, :] = q
        qk_ref[0, 0, j, CH:, :] = k
        grams = mm(jnp.concatenate([q, k], axis=0), k, NT)
        for r in range(rep):
            h = j * rep + r
            spread = log_col[:, h : h + 1] - log_row[h : h + 1, :]
            ratio = jnp.exp(jnp.where(upto, spread, -1e30))
            gram_ref[0, 0, h] = (grams[:CH] * ratio).astype(BF16)
            lower.append(jnp.where(strict, beta_col[:, h : h + 1] * ratio * grams[CH:], 0.0))
    eye = jnp.where(rows == cols, 1.0, 0.0).astype(F32)
    first = strict & (apart == 1)
    inv = [eye - jnp.where(first, low, 0.0) for low in lower]
    level = 1
    while (1 << level) < CH:
        pick = strict & ((apart >> level) == 1)
        inv16 = [t.astype(BF16) for t in inv]
        mid = [mm(jnp.where(pick, low, 0.0).astype(BF16), t) for low, t in zip(lower, inv16)]
        inv = [t - mm(t16, x.astype(BF16)) for t, t16, x in zip(inv, inv16, mid)]
        level += 1
    for h in range(heads):
        off = jnp.where(strict, inv[h], 0.0) * beta_row[h : h + 1, :]
        solve_ref[0, 0, h] = off.astype(BF16)


def advance(qk, vals, solve, gram, logs, beta_cols, states):
    reads = mm(qk, jnp.concatenate([s.astype(BF16) for s in states], axis=1))
    outs, tails = [], []
    for r, state in enumerate(states):
        fade = jnp.exp(logs[r])
        part = reads[:, r * DV : (r + 1) * DV]
        resid = vals[r].astype(F32) - fade * part[CH:]
        new = beta_cols[r] * resid + mm(solve[r], resid.astype(BF16))
        outs.append(fade * part[:CH] + mm(gram[r], new.astype(BF16)))
        tails.append((jnp.exp(logs[r][CH - 1 :, :] - logs[r]) * new).astype(BF16))
    grown = mm(qk[CH:], jnp.concatenate(tails, axis=1), TN)
    states = [
        jnp.exp(logs[r][CH - 1 :, :]) * s + grown[:, r * DV : (r + 1) * DV]
        for r, s in enumerate(states)
    ]
    return outs, states


def norm_rows(o, gain):
    return o * lax.rsqrt(jnp.mean(o * o, axis=-1, keepdims=True) + EPS_NORM) * gain


def seq_kernel(
    rep, keep, owner_ref, length_ref, qk_ref, v_ref, solve_ref, gram_ref,
    beta_ref, decay_ref, seed_ref, gain_ref, out_ref, *end_ref
):
    spans, key_heads = qk_ref.shape[1], qk_ref.shape[2]
    heads = key_heads * rep
    length = length_ref[pl.program_id(0)]
    gain = gain_ref[...]
    states = [seed_ref[0, h] for h in range(heads)]
    place = lax.broadcasted_iota(jnp.int32, (CH, DV), 0)
    for c in range(spans):
        span = slice(c * CH, (c + 1) * CH)
        log_col = running_log(decay_ref[0, :, span]).T
        beta_col = beta_ref[0, :, span].T
        live = place + c * CH < length
        for j in range(key_heads):
            hs = range(j * rep, (j + 1) * rep)
            outs, grown = advance(
                qk_ref[0, c, j],
                [v_ref[0, span, h * DV : (h + 1) * DV] for h in hs],
                [solve_ref[0, c, h] for h in hs],
                [gram_ref[0, c, h] for h in hs],
                [log_col[:, h : h + 1] for h in hs],
                [beta_col[:, h : h + 1] for h in hs],
                [states[h] for h in hs],
            )
            for h, o, s in zip(hs, outs, grown):
                states[h] = s
                out_ref[0, span, h * DV : (h + 1) * DV] = jnp.where(
                    live, norm_rows(o, gain), 0.0
                ).astype(BF16)
    if keep:
        for h in range(heads):
            end_ref[0][0, h] = states[h]


def group_of(key_heads):
    return 4 if key_heads % 4 == 0 else key_heads


PARAMS = dict(vmem_limit_bytes=48 * 1024 * 1024)


def prepare(q, k, beta, decay):
    slots, tokens, width = q.shape
    key_heads, heads = width // DK, beta.shape[1]
    rep, g, spans = heads // key_heads, group_of(width // DK), tokens // CH
    gate = pl.BlockSpec((1, g * rep, CH), lambda s, c, j: (s, j, c))
    rows = pl.BlockSpec((1, CH, g * DK), lambda s, c, j: (s, c, j))
    square = pl.BlockSpec((1, 1, g * rep, CH, CH), lambda s, c, j: (s, c, j, 0, 0))
    return pl.pallas_call(
        functools.partial(pre_kernel, rep),
        grid=(slots, spans, key_heads // g),
        in_specs=[rows, rows, gate, gate],
        out_specs=[
            pl.BlockSpec((1, 1, g, 2 * CH, DK), lambda s, c, j: (s, c, j, 0, 0)),
            square,
            square,
        ],
        out_shape=[
            jax.ShapeDtypeStruct((slots, spans, key_heads, 2 * CH, DK), BF16),
            jax.ShapeDtypeStruct((slots, spans, heads, CH, CH), BF16),
            jax.ShapeDtypeStruct((slots, spans, heads, CH, CH), BF16),
        ],
        compiler_params=pltpu.CompilerParams(**PARAMS),
        cost_estimate=pl.CostEstimate(
            flops=slots * tokens * heads * CH * CH * 30, bytes_accessed=slots * tokens * heads * 800,
            transcendentals=slots * tokens * heads * CH,
        ),
        name="prepare",
    )(q, k, beta, decay)


def sweep(terms, v, beta, decay, seeds, owner, length, gain, keep):
    qk, solve, gram = terms
    slots, spans, key_heads = qk.shape[:3]
    heads = beta.shape[1]
    rep, g, tokens = heads // key_heads, group_of(key_heads), spans * CH
    gate = pl.BlockSpec((1, g * rep, tokens), lambda s, j, *_: (s, j, 0))
    vals = pl.BlockSpec((1, tokens, g * rep * DV), lambda s, j, *_: (s, 0, j))
    square = pl.BlockSpec((1, spans, g * rep, CH, CH), lambda s, j, *_: (s, 0, j, 0, 0))
    out_specs, out_shape = [vals], [jax.ShapeDtypeStruct(v.shape, BF16)]
    if keep:
        out_specs.append(pl.BlockSpec((1, g * rep, DK, DV), lambda s, j, *_: (s, j, 0, 0)))
        out_shape.append(jax.ShapeDtypeStruct((slots, heads, DK, DV), F32))
    return pl.pallas_call(
        functools.partial(seq_kernel, rep, keep),
        grid_spec=pltpu.PrefetchScalarGridSpec(
            num_scalar_prefetch=2,
            grid=(slots, key_heads // g),
            in_specs=[
                pl.BlockSpec((1, spans, g, 2 * CH, DK), lambda s, j, *_: (s, 0, j, 0, 0)),
                vals,
                square,
                square,
                gate,
                gate,
                pl.BlockSpec((1, g * rep, DK, DV), lambda s, j, own, _: (own[s], j, 0, 0)),
                pl.BlockSpec((1, DV), lambda s, j, *_: (0, 0)),
            ],
            out_specs=out_specs,
        ),
        out_shape=out_shape,
        compiler_params=pltpu.CompilerParams(**PARAMS),
        name="sweep",
    )(owner, length, qk, v, solve, gram, beta, decay, seeds, gain)


def from_behind(value, axis):
    count = lax.axis_size(axis)
    return lax.ppermute(value, axis, [(i, i + 1) for i in range(count - 1)])


def slot_facts(slot_branch, branch_length, branch_prompt, slot_count):
    rank = lax.axis_index("seq") * lax.axis_size("prompt") + lax.axis_index("prompt")
    slot_ids = rank * slot_count + jnp.arange(slot_count, dtype=jnp.int32)
    branch_ids = jnp.arange(slot_branch.shape[0], dtype=jnp.int32)
    mine = jnp.sum(
        jnp.where(slot_ids[:, None] == branch_ids[None, :], slot_branch[None, :], 0), axis=1
    )
    hit = mine[:, None] == branch_ids[None, :]
    length = jnp.sum(jnp.where(hit, branch_length[None, :], 0), axis=1)
    owner = jnp.sum(jnp.where(hit, branch_prompt[None, :], 0), axis=1)
    return length, owner


def local(
    prompt_queries, prompt_keys, prompt_values, prompt_beta, prompt_decay,
    suffix_queries, suffix_keys, suffix_values, suffix_beta, suffix_decay,
    norm_gain, slot_branch, branch_length, branch_prompt,
):
    gain = norm_gain[None, :]
    length, owner = slot_facts(slot_branch, branch_length, branch_prompt, suffix_queries.shape[0])
    terms = prepare(prompt_queries, prompt_keys, prompt_beta, prompt_decay)
    heads = prompt_beta.shape[1]
    whole = jnp.full((1,), prompt_queries.shape[1], jnp.int32)
    zero = jnp.zeros((1,), jnp.int32)
    state = jnp.zeros((1, heads, DK, DV), F32)
    count = lax.axis_size("seq")
    for step in range(count):
        prompt_out, state_out = sweep(
            terms, prompt_values, prompt_beta, prompt_decay, state, zero, whole, gain, True
        )
        if step < count - 1:
            state = from_behind(state_out, "seq")
    final = jnp.where(lax.axis_index("seq") == count - 1, state_out, 0.0)
    final = lax.psum(final, "seq")
    finals = lax.all_gather(final, "prompt", axis=0, tiled=True)
    suffix_terms = prepare(suffix_queries, suffix_keys, suffix_beta, suffix_decay)
    suffix_out = sweep(
        suffix_terms, suffix_values, suffix_beta, suffix_decay, finals, owner, length, gain, False
    )[0]
    return (prompt_out, suffix_out)


def solution(mesh):
    lead = P(("groups", "prompt"), "seq", "head")
    lead_gate = P(("groups", "prompt"), "head", "seq")
    slot = P(("groups", "seq", "prompt"), None, "head")
    slot_gate = P(("groups", "seq", "prompt"), "head", None)
    return jax.shard_map(
        local,
        mesh=mesh,
        in_specs=(
            lead, lead, lead, lead_gate, lead_gate, slot, slot, slot, slot_gate, slot_gate,
            P(), P("groups"), P("groups"), P("groups"),
        ),
        out_specs=(lead, slot),
        check_vma=False,
    )
```

```python
import functools

import jax
import jax.numpy as jnp
from jax import lax
from jax.experimental import pallas as pl
from jax.experimental.pallas import tpu as pltpu
from jax.sharding import PartitionSpec as P

DK = 128
DV = 128
CH = 128
EPS_NORM = 1e-06
F32 = jnp.float32
BF16 = jnp.bfloat16
NN = (((1,), (0,)), ((), ()))
NT = (((1,), (1,)), ((), ()))
TN = (((0,), (0,)), ((), ()))


def mm(a, b, dims=NN):
    return lax.dot_general(a, b, dims, preferred_element_type=F32)


def unit(x):
    w = x.astype(F32)
    return (w * lax.rsqrt(jnp.sum(w * w, axis=-1, keepdims=True) + EPS_NORM)).astype(BF16)


def iotas():
    return (
        lax.broadcasted_iota(jnp.int32, (CH, CH), 0),
        lax.broadcasted_iota(jnp.int32, (CH, CH), 1),
    )


def running_log(decay):
    rows, cols = iotas()
    tri = jnp.where(rows <= cols, 1.0, 0.0).astype(F32)
    return lax.dot_general(
        decay, tri, NN, precision=lax.Precision.HIGHEST, preferred_element_type=F32
    )


def gate_columns(log_col, beta_col, j, rep):
    hs = slice(j * rep, (j + 1) * rep)
    return jnp.concatenate([log_col[:, hs], beta_col[:, hs]], axis=1)


def gate_rows(log_row, beta_row, j, rep):
    hs = slice(j * rep, (j + 1) * rep)
    return jnp.concatenate([log_row[hs], beta_row[hs]], axis=0)


def solve_spans(rep, queries, keys, gates_row, gates_col):
    rows, cols = iotas()
    upto = rows >= cols
    strict = rows > cols
    apart = rows ^ cols
    pairs, weights, lower = [], [], []
    for q, k, row, col in zip(queries, keys, gates_row, gates_col):
        q, k = unit(q), unit(k)
        pair = jnp.concatenate([q, k], axis=0)
        pairs.append(pair)
        grams = mm(pair, k, NT)
        for r in range(rep):
            spread = col[:, r : r + 1] - row[r : r + 1, :]
            ratio = jnp.exp(jnp.where(upto, spread, -1e30))
            weights.append((grams[:CH] * ratio).astype(BF16))
            beta = col[:, rep + r : rep + r + 1]
            lower.append(jnp.where(strict, beta * ratio * grams[CH:], 0.0))
    eye = jnp.where(rows == cols, 1.0, 0.0).astype(F32)
    first = strict & (apart == 1)
    inv = [eye - jnp.where(first, low, 0.0) for low in lower]
    level = 1
    while (1 << level) < CH:
        pick = strict & ((apart >> level) == 1)
        inv16 = [t.astype(BF16) for t in inv]
        mid = [mm(jnp.where(pick, low, 0.0).astype(BF16), t) for low, t in zip(lower, inv16)]
        inv = [t - mm(t16, x.astype(BF16)) for t, t16, x in zip(inv, inv16, mid)]
        level += 1
    solves = []
    for h, t in enumerate(inv):
        row = gates_row[h // rep]
        r = rep + h % rep
        solves.append((jnp.where(strict, t, 0.0) * row[r : r + 1, :]).astype(BF16))
    return pairs, weights, solves


def pre_kernel(rep, q_ref, k_ref, beta_ref, decay_ref, qk_ref, solve_ref, gram_ref, cols_ref):
    key_heads = q_ref.shape[2] // DK
    log_row = running_log(decay_ref[0])
    log_col = log_row.T
    beta_row = beta_ref[0]
    beta_col = beta_row.T
    span = range(key_heads)
    cols = [gate_columns(log_col, beta_col, j, rep) for j in span]
    pairs, weights, solves = solve_spans(
        rep,
        [q_ref[0, :, j * DK : (j + 1) * DK] for j in span],
        [k_ref[0, :, j * DK : (j + 1) * DK] for j in span],
        [gate_rows(log_row, beta_row, j, rep) for j in span],
        cols,
    )
    for j in span:
        qk_ref[0, 0, j] = pairs[j]
        cols_ref[0, 0, j] = cols[j]
    for h in range(key_heads * rep):
        gram_ref[0, 0, h] = weights[h]
        solve_ref[0, 0, h] = solves[h]


def advance(qk, vals, solve, gram, logs, beta_cols, states):
    reads = mm(qk, jnp.concatenate([s.astype(BF16) for s in states], axis=1))
    outs, tails = [], []
    for r, state in enumerate(states):
        fade = jnp.exp(logs[r])
        part = reads[:, r * DV : (r + 1) * DV]
        resid = vals[r].astype(F32) - fade * part[CH:]
        new = beta_cols[r] * resid + mm(solve[r], resid.astype(BF16))
        outs.append(fade * part[:CH] + mm(gram[r], new.astype(BF16)))
        tails.append((jnp.exp(logs[r][CH - 1 :, :] - logs[r]) * new).astype(BF16))
    grown = mm(qk[CH:], jnp.concatenate(tails, axis=1), TN)
    states = [
        jnp.exp(logs[r][CH - 1 :, :]) * s + grown[:, r * DV : (r + 1) * DV]
        for r, s in enumerate(states)
    ]
    return outs, states


def norm_rows(o, gain):
    return o * lax.rsqrt(jnp.mean(o * o, axis=-1, keepdims=True) + EPS_NORM) * gain


def seq_kernel(
    rep, owner_ref, length_ref, qk_ref, v_ref, solve_ref, gram_ref, cols_ref, seed_ref,
    gain_ref, out_ref
):
    spans, key_heads = qk_ref.shape[1], qk_ref.shape[2]
    heads = key_heads * rep
    length = length_ref[pl.program_id(0)]
    gain = gain_ref[...]
    states = [seed_ref[0, h] for h in range(heads)]
    place = lax.broadcasted_iota(jnp.int32, (CH, DV), 0)
    for c in range(spans):
        span = slice(c * CH, (c + 1) * CH)
        live = place + c * CH < length
        for j in range(key_heads):
            hs = range(j * rep, (j + 1) * rep)
            cols = cols_ref[0, c, j]
            outs, grown = advance(
                qk_ref[0, c, j],
                [v_ref[0, span, h * DV : (h + 1) * DV] for h in hs],
                [solve_ref[0, c, h] for h in hs],
                [gram_ref[0, c, h] for h in hs],
                [cols[:, r : r + 1] for r in range(rep)],
                [cols[:, rep + r : rep + r + 1] for r in range(rep)],
                [states[h] for h in hs],
            )
            for h, o, s in zip(hs, outs, grown):
                states[h] = s
                out_ref[0, span, h * DV : (h + 1) * DV] = jnp.where(
                    live, norm_rows(o, gain), 0.0
                ).astype(BF16)


def relay_kernel(
    rep, pqk, pv, psolve, pgram, pcols, gain_ref, *rest
):
    if len(rest) == 10:
        work, rest = None, rest
    else:
        work, rest = rest[:4] + rest[6:10] + rest[12:13], rest[4:6] + rest[10:12] + rest[13:]
    pout, finals, inbox, outbox, fsend, frecv, bsend, brecv, csend, crecv = rest
    key_heads = pqk.shape[2]
    rank, last = lax.axis_index("seq"), lax.axis_size("seq") - 1
    mine = lax.axis_index("prompt")
    other = 1 - mine
    gain = gain_ref[...]
    items = 0
    if work is not None:
        sq, sk, sbeta, sdecay, sqk, ssolve, sgram, scols, srows = work
        slots, spans = sqk.shape[0], sqk.shape[1]
        pack = 2 if key_heads % 2 == 0 else 1
        packs = key_heads // pack
        items = slots * spans * packs

    def forward(i):
        return pltpu.make_async_remote_copy(
            src_ref=outbox.at[i], dst_ref=inbox.at[i], send_sem=fsend.at[i],
            recv_sem=frecv.at[i], device_id={"seq": rank + 1}, device_id_type=pl.DeviceIdType.MESH,
        )

    def block(p, i):
        return finals.at[p, pl.ds(i * rep, rep)]

    def backward(i):
        return pltpu.make_async_remote_copy(
            src_ref=block(mine, i), dst_ref=block(mine, i), send_sem=bsend.at[i],
            recv_sem=brecv.at[i], device_id={"seq": rank - 1}, device_id_type=pl.DeviceIdType.MESH,
        )

    def across(p, i):
        return pltpu.make_async_remote_copy(
            src_ref=block(p, i), dst_ref=block(p, i), send_sem=csend.at[i],
            recv_sem=crecv.at[i], device_id={"prompt": other}, device_id_type=pl.DeviceIdType.MESH,
        )

    barrier = pltpu.get_barrier_semaphore()

    def greet(where):
        pl.semaphore_signal(barrier, inc=1, device_id=where, device_id_type=pl.DeviceIdType.MESH)

    greet({"prompt": other})

    @pl.when(rank > 0)
    def _():
        greet({"seq": rank - 1})

    @pl.when(rank < last)
    def _():
        greet({"seq": rank + 1})

    pl.semaphore_wait(
        barrier, 1 + jnp.where(rank > 0, 1, 0) + jnp.where(rank < last, 1, 0)
    )

    @pl.when(rank == 0)
    def _():
        inbox[...] = jnp.zeros_like(inbox)

    if work is not None:
        for s in range(slots):
            for c in range(spans):
                span = slice(c * CH, (c + 1) * CH)
                log_row = running_log(sdecay[s, :, span])
                beta_row = sbeta[s, :, span]
                log_col, beta_col = log_row.T, beta_row.T
                for j in range(key_heads):
                    scols[s, c, j] = gate_columns(log_col, beta_col, j, rep)
                    srows[s, c, j] = gate_rows(log_row, beta_row, j, rep)

    def step_forward(i):
        @pl.when(rank > 0)
        def _():
            forward(i).wait_recv()

        at = pl.ds(pl.multiple_of(i * rep * DV, rep * DV), rep * DV)
        v = pv[0, :, at]
        cols = pcols[0, 0, i]
        outs, grown = advance(
            pqk[0, 0, i],
            [v[:, r * DV : (r + 1) * DV] for r in range(rep)],
            [psolve[0, 0, i * rep + r] for r in range(rep)],
            [pgram[0, 0, i * rep + r] for r in range(rep)],
            [cols[:, r : r + 1] for r in range(rep)],
            [cols[:, rep + r : rep + r + 1] for r in range(rep)],
            [inbox[i, r] for r in range(rep)],
        )

        @pl.when(rank < last)
        def _():
            for r in range(rep):
                outbox[i, r] = grown[r]
            forward(i).start()

        @pl.when(rank == last)
        def _():
            for r in range(rep):
                finals[mine, i * rep + r] = grown[r]

        pout[0, :, at] = jnp.concatenate(
            [norm_rows(o, gain).astype(BF16) for o in outs], axis=1
        )

    def step_back(i):
        @pl.when(rank < last)
        def _():
            backward(i).wait_recv()

        @pl.when(rank > 0)
        def _():
            backward(i).start()

        across(mine, i).start()

    def step_work(m):
        place, g = m // packs, m % packs
        s, c = place // spans, place % spans
        rows = pl.ds(pl.multiple_of(c * CH, CH), CH)
        at = pl.ds(pl.multiple_of(g * pack * DK, pack * DK), pack * DK)
        q, k = sq[s, rows, at], sk[s, rows, at]
        pairs, weights, solves = solve_spans(
            rep,
            [q[:, j * DK : (j + 1) * DK] for j in range(pack)],
            [k[:, j * DK : (j + 1) * DK] for j in range(pack)],
            [srows[s, c, g * pack + j] for j in range(pack)],
            [scols[s, c, g * pack + j] for j in range(pack)],
        )
        for j in range(pack):
            sqk[s, c, g * pack + j] = pairs[j]
        for h in range(pack * rep):
            sgram[s, c, g * pack * rep + h] = weights[h]
            ssolve[s, c, g * pack * rep + h] = solves[h]

    first_at = LAG * rank
    back_at = LAG * last + (LAG + 1) * (last - rank)

    def tick(t, carry):
        i = t - first_at
        pl.when((i >= 0) & (i < key_heads))(lambda: step_forward(i))
        j = t - back_at
        pl.when((j >= 0) & (j < key_heads))(lambda: step_back(j))
        if work is not None:
            pl.when(t < items)(lambda: step_work(t))
        return carry

    lax.fori_loop(0, max(items, (2 * LAG + 1) * last + key_heads), tick, 0)

    def finish(i, carry):
        @pl.when(rank < last)
        def _():
            forward(i).wait_send()

        @pl.when(rank > 0)
        def _():
            backward(i).wait_send()

        across(mine, i).wait_send()
        across(other, i).wait_recv()
        return carry

    lax.fori_loop(0, key_heads, finish, 0)


LAG = 2
OVERLAP = True


def group_of(key_heads):
    return 4 if key_heads % 4 == 0 else key_heads


PARAMS = dict(vmem_limit_bytes=48 * 1024 * 1024)


def prepare(q, k, beta, decay):
    slots, tokens, width = q.shape
    key_heads, heads = width // DK, beta.shape[1]
    rep, g, spans = heads // key_heads, group_of(width // DK), tokens // CH
    gate = pl.BlockSpec((1, g * rep, CH), lambda s, c, j: (s, j, c))
    rows = pl.BlockSpec((1, CH, g * DK), lambda s, c, j: (s, c, j))
    square = pl.BlockSpec((1, 1, g * rep, CH, CH), lambda s, c, j: (s, c, j, 0, 0))
    return pl.pallas_call(
        functools.partial(pre_kernel, rep),
        grid=(slots, spans, key_heads // g),
        in_specs=[rows, rows, gate, gate],
        out_specs=[
            pl.BlockSpec((1, 1, g, 2 * CH, DK), lambda s, c, j: (s, c, j, 0, 0)),
            square,
            square,
            pl.BlockSpec((1, 1, g, CH, 2 * rep), lambda s, c, j: (s, c, j, 0, 0)),
        ],
        out_shape=[
            jax.ShapeDtypeStruct((slots, spans, key_heads, 2 * CH, DK), BF16),
            jax.ShapeDtypeStruct((slots, spans, heads, CH, CH), BF16),
            jax.ShapeDtypeStruct((slots, spans, heads, CH, CH), BF16),
            jax.ShapeDtypeStruct((slots, spans, key_heads, CH, 2 * rep), F32),
        ],
        compiler_params=pltpu.CompilerParams(**PARAMS),
        cost_estimate=pl.CostEstimate(
            flops=slots * tokens * heads * CH * CH * 30, bytes_accessed=slots * tokens * heads * 800,
            transcendentals=slots * tokens * heads * CH,
        ),
        name="prepare",
    )(q, k, beta, decay)


def relay(terms, v, gain, suffix):
    key_heads, heads = terms[0].shape[2], terms[1].shape[2]
    rep = heads // key_heads
    count = lax.axis_size("prompt")
    vmem = pl.BlockSpec(memory_space=pltpu.VMEM)
    outs = [
        jax.ShapeDtypeStruct(v.shape, BF16),
        jax.ShapeDtypeStruct((count, heads, DK, DV), F32),
    ]
    scratch = [
        pltpu.VMEM((key_heads, rep, DK, DV), F32),
        pltpu.VMEM((key_heads, rep, DK, DV), F32),
    ] + [pltpu.SemaphoreType.DMA((key_heads,))] * 6
    args = [terms[0], v, terms[1], terms[2], terms[3], gain]
    body = functools.partial(relay_kernel, rep)
    if suffix is not None:
        q, k, beta, decay = suffix
        slots, spans = q.shape[0], q.shape[1] // CH
        work_outs = [
            jax.ShapeDtypeStruct((slots, spans, key_heads, 2 * CH, DK), BF16),
            jax.ShapeDtypeStruct((slots, spans, heads, CH, CH), BF16),
            jax.ShapeDtypeStruct((slots, spans, heads, CH, CH), BF16),
            jax.ShapeDtypeStruct((slots, spans, key_heads, CH, 2 * rep), F32),
        ]
        args += list(suffix)
        outs = outs + work_outs
        scratch = scratch[:2] + [pltpu.VMEM((slots, spans, key_heads, 2 * rep, CH), F32)] + scratch[2:]
    return pl.pallas_call(
        body,
        out_shape=outs,
        in_specs=[vmem] * len(args),
        out_specs=[vmem] * len(outs),
        scratch_shapes=scratch,
        compiler_params=pltpu.CompilerParams(
            collective_id=0, has_side_effects=True, vmem_limit_bytes=56 * 1024 * 1024
        ),
        name="relay",
    )(*args)


def sweep(terms, v, seeds, owner, length, gain):
    qk, solve, gram, cols = terms
    slots, spans, key_heads = qk.shape[:3]
    heads = solve.shape[2]
    rep, g, tokens = heads // key_heads, group_of(key_heads), spans * CH
    vals = pl.BlockSpec((1, tokens, g * rep * DV), lambda s, j, *_: (s, 0, j))
    square = pl.BlockSpec((1, spans, g * rep, CH, CH), lambda s, j, *_: (s, 0, j, 0, 0))
    return pl.pallas_call(
        functools.partial(seq_kernel, rep),
        grid_spec=pltpu.PrefetchScalarGridSpec(
            num_scalar_prefetch=2,
            grid=(slots, key_heads // g),
            in_specs=[
                pl.BlockSpec((1, spans, g, 2 * CH, DK), lambda s, j, *_: (s, 0, j, 0, 0)),
                vals,
                square,
                square,
                pl.BlockSpec((1, spans, g, CH, 2 * rep), lambda s, j, *_: (s, 0, j, 0, 0)),
                pl.BlockSpec((1, g * rep, DK, DV), lambda s, j, own, _: (own[s], j, 0, 0)),
                pl.BlockSpec((1, DV), lambda s, j, *_: (0, 0)),
            ],
            out_specs=vals,
        ),
        out_shape=jax.ShapeDtypeStruct(v.shape, BF16),
        compiler_params=pltpu.CompilerParams(**PARAMS),
        name="sweep",
    )(owner, length, qk, v, solve, gram, cols, seeds, gain)


def slot_facts(slot_branch, branch_length, branch_prompt, slot_count):
    rank = lax.axis_index("seq") * lax.axis_size("prompt") + lax.axis_index("prompt")
    slot_ids = rank * slot_count + jnp.arange(slot_count, dtype=jnp.int32)
    branch_ids = jnp.arange(slot_branch.shape[0], dtype=jnp.int32)
    mine = jnp.sum(
        jnp.where(slot_ids[:, None] == branch_ids[None, :], slot_branch[None, :], 0), axis=1
    )
    hit = mine[:, None] == branch_ids[None, :]
    length = jnp.sum(jnp.where(hit, branch_length[None, :], 0), axis=1)
    owner = jnp.sum(jnp.where(hit, branch_prompt[None, :], 0), axis=1)
    return length, owner


def local(
    prompt_queries, prompt_keys, prompt_values, prompt_beta, prompt_decay,
    suffix_queries, suffix_keys, suffix_values, suffix_beta, suffix_decay,
    norm_gain, slot_branch, branch_length, branch_prompt,
):
    gain = norm_gain[None, :]
    length, owner = slot_facts(slot_branch, branch_length, branch_prompt, suffix_queries.shape[0])
    terms = prepare(prompt_queries, prompt_keys, prompt_beta, prompt_decay)
    if OVERLAP:
        suffix = (suffix_queries, suffix_keys, suffix_beta, suffix_decay)
        prompt_out, finals, *suffix_terms = relay(terms, prompt_values, gain, suffix)
    else:
        prompt_out, finals = relay(terms, prompt_values, gain, None)
        suffix_terms = prepare(suffix_queries, suffix_keys, suffix_beta, suffix_decay)
    suffix_out = sweep(suffix_terms, suffix_values, finals, owner, length, gain)
    return (prompt_out, suffix_out)


def solution(mesh):
    lead = P(("groups", "prompt"), "seq", "head")
    lead_gate = P(("groups", "prompt"), "head", "seq")
    slot = P(("groups", "seq", "prompt"), None, "head")
    slot_gate = P(("groups", "seq", "prompt"), "head", None)
    return jax.shard_map(
        local,
        mesh=mesh,
        in_specs=(
            lead, lead, lead, lead_gate, lead_gate, slot, slot, slot, slot_gate, slot_gate,
            P(), P("groups"), P("groups"), P("groups"),
        ),
        out_specs=(lead, slot),
        check_vma=False,
    )
```

```python
import functools

import jax
import jax.numpy as jnp
from jax import lax
from jax.experimental import pallas as pl
from jax.experimental.pallas import tpu as pltpu
from jax.sharding import PartitionSpec as P

DK = 128
DV = 128
CH = 128
EPS_NORM = 1e-06
F32 = jnp.float32
BF16 = jnp.bfloat16
NN = (((1,), (0,)), ((), ()))
NT = (((1,), (1,)), ((), ()))
TN = (((0,), (0,)), ((), ()))


def mm(a, b, dims=NN):
    return lax.dot_general(a, b, dims, preferred_element_type=F32)


def unit(x):
    w = x.astype(F32)
    return (w * lax.rsqrt(jnp.sum(w * w, axis=-1, keepdims=True) + EPS_NORM)).astype(BF16)


def iotas():
    return (
        lax.broadcasted_iota(jnp.int32, (CH, CH), 0),
        lax.broadcasted_iota(jnp.int32, (CH, CH), 1),
    )


def running_log(decay):
    rows, cols = iotas()
    tri = jnp.where(rows <= cols, 1.0, 0.0).astype(F32)
    return lax.dot_general(
        decay, tri, NN, precision=lax.Precision.HIGHEST, preferred_element_type=F32
    )


def gate_columns(log_col, beta_col, j, rep):
    hs = slice(j * rep, (j + 1) * rep)
    return jnp.concatenate([log_col[:, hs], beta_col[:, hs]], axis=1)


def gate_rows(log_row, beta_row, j, rep):
    hs = slice(j * rep, (j + 1) * rep)
    return jnp.concatenate([log_row[hs], beta_row[hs]], axis=0)


def solve_spans(rep, queries, keys, gates_row, gates_col):
    rows, cols = iotas()
    upto = rows >= cols
    strict = rows > cols
    apart = rows ^ cols
    pairs, weights, lower = [], [], []
    for q, k, row, col in zip(queries, keys, gates_row, gates_col):
        q, k = unit(q), unit(k)
        pair = jnp.concatenate([q, k], axis=0)
        pairs.append(pair)
        grams = mm(pair, k, NT)
        for r in range(rep):
            spread = col[:, r : r + 1] - row[r : r + 1, :]
            ratio = jnp.exp(jnp.where(upto, spread, -1e30))
            weights.append((grams[:CH] * ratio).astype(BF16))
            beta = col[:, rep + r : rep + r + 1]
            lower.append(jnp.where(strict, beta * ratio * grams[CH:], 0.0))
    eye = jnp.where(rows == cols, 1.0, 0.0).astype(F32)
    first = strict & (apart == 1)
    inv = [eye - jnp.where(first, low, 0.0) for low in lower]
    level = 1
    while (1 << level) < CH:
        size = 1 << level
        pick = strict & ((apart >> level) == 1)
        inv16 = [t.astype(BF16) for t in inv]
        if size < HALF_FROM:
            mid = [mm(jnp.where(pick, low, 0.0).astype(BF16), t) for low, t in zip(lower, inv16)]
            inv = [t - mm(t16, x.astype(BF16)) for t, t16, x in zip(inv, inv16, mid)]
        else:
            starts = range(0, CH, 2 * size)

            def odd(x):
                return jnp.concatenate([x[i + size : i + 2 * size] for i in starts], axis=0)

            def spread_odd(x, fill):
                parts = []
                for n, i in enumerate(starts):
                    parts += [fill[i : i + size], x[n * size : (n + 1) * size]]
                return jnp.concatenate(parts, axis=0)

            blank = jnp.zeros((CH, CH), BF16)
            chosen = odd(pick.astype(F32)) > 0
            mid = [
                mm(jnp.where(chosen, odd(low), 0.0).astype(BF16), t)
                for low, t in zip(lower, inv16)
            ]
            inv = [
                spread_odd(odd(t) - mm(odd(t16), spread_odd(x.astype(BF16), blank)), t)
                for t, t16, x in zip(inv, inv16, mid)
            ]
        level += 1
    solves = []
    for h, t in enumerate(inv):
        row = gates_row[h // rep]
        r = rep + h % rep
        solves.append((jnp.where(strict, t, 0.0) * row[r : r + 1, :]).astype(BF16))
    return pairs, weights, solves


def pre_kernel(rep, q_ref, k_ref, beta_ref, decay_ref, qk_ref, solve_ref, gram_ref, cols_ref):
    key_heads = q_ref.shape[2] // DK
    log_row = running_log(decay_ref[0])
    log_col = log_row.T
    beta_row = beta_ref[0]
    beta_col = beta_row.T
    span = range(key_heads)
    cols = [gate_columns(log_col, beta_col, j, rep) for j in span]
    pairs, weights, solves = solve_spans(
        rep,
        [q_ref[0, :, j * DK : (j + 1) * DK] for j in span],
        [k_ref[0, :, j * DK : (j + 1) * DK] for j in span],
        [gate_rows(log_row, beta_row, j, rep) for j in span],
        cols,
    )
    for j in span:
        qk_ref[0, 0, j] = pairs[j]
        cols_ref[0, 0, j] = cols[j]
    for h in range(key_heads * rep):
        gram_ref[0, 0, h] = weights[h]
        solve_ref[0, 0, h] = solves[h]


def advance(rep, entries):
    heads = [(n, r) for n in range(len(entries)) for r in range(rep)]
    reads = [
        mm(e[0], jnp.concatenate([s.astype(BF16) for s in e[5]], axis=1)) for e in entries
    ]
    fades = [jnp.exp(entries[n][4][:, r : r + 1]) for n, r in heads]
    parts = [reads[n][:, r * DV : (r + 1) * DV] for n, r in heads]
    resids = [
        entries[n][1][r].astype(F32) - fade * part[CH:]
        for (n, r), fade, part in zip(heads, fades, parts)
    ]
    news = [
        entries[n][4][:, rep + r : rep + r + 1] * resid
        + mm(entries[n][2][r], resid.astype(BF16))
        for (n, r), resid in zip(heads, resids)
    ]
    ends = [entries[n][4][CH - 1 :, r : r + 1] for n, r in heads]
    tails = [
        (jnp.exp(end - entries[n][4][:, r : r + 1]) * new).astype(BF16)
        for (n, r), end, new in zip(heads, ends, news)
    ]
    grown = [
        mm(e[0][CH:], jnp.concatenate(tails[n * rep : (n + 1) * rep], axis=1), TN)
        for n, e in enumerate(entries)
    ]
    states = [
        jnp.exp(end) * entries[n][5][r] + grown[n][:, r * DV : (r + 1) * DV]
        for (n, r), end in zip(heads, ends)
    ]
    outs = [
        fade * part[:CH] + mm(entries[n][3][r], new.astype(BF16))
        for (n, r), fade, part, new in zip(heads, fades, parts, news)
    ]
    return outs, states


def norm_rows(o, gain):
    return o * lax.rsqrt(jnp.mean(o * o, axis=-1, keepdims=True) + EPS_NORM) * gain


def seq_kernel(
    rep, owner_ref, length_ref, qk_ref, v_ref, solve_ref, gram_ref, cols_ref, seed_ref,
    gain_ref, out_ref
):
    spans, key_heads = qk_ref.shape[1], qk_ref.shape[2]
    heads = key_heads * rep
    length = length_ref[pl.program_id(0)]
    gain = gain_ref[...]
    states = [seed_ref[0, h] for h in range(heads)]
    place = lax.broadcasted_iota(jnp.int32, (CH, DV), 0)
    for c in range(spans):
        span = slice(c * CH, (c + 1) * CH)
        live = place + c * CH < length
        outs, states = advance(
            rep,
            [
                (
                    qk_ref[0, c, j],
                    [v_ref[0, span, h * DV : (h + 1) * DV] for h in range(j * rep, (j + 1) * rep)],
                    [solve_ref[0, c, h] for h in range(j * rep, (j + 1) * rep)],
                    [gram_ref[0, c, h] for h in range(j * rep, (j + 1) * rep)],
                    cols_ref[0, c, j],
                    states[j * rep : (j + 1) * rep],
                )
                for j in range(key_heads)
            ],
        )
        for h, o in enumerate(outs):
            out_ref[0, span, h * DV : (h + 1) * DV] = jnp.where(
                live, norm_rows(o, gain), 0.0
            ).astype(BF16)


def relay_kernel(
    rep, pqk, pv, psolve, pgram, pcols, gain_ref, *rest
):
    if len(rest) == 10:
        work, rest = None, rest
    else:
        work, rest = rest[:4] + rest[6:10] + rest[12:13], rest[4:6] + rest[10:12] + rest[13:]
    pout, finals, inbox, outbox, fsend, frecv, bsend, brecv, csend, crecv = rest
    key_heads = pqk.shape[2]
    rank, last = lax.axis_index("seq"), lax.axis_size("seq") - 1
    mine = lax.axis_index("prompt")
    other = 1 - mine
    gain = gain_ref[...]
    items = 0
    if work is not None:
        sq, sk, sbeta, sdecay, sqk, ssolve, sgram, scols, srows = work
        slots, spans = sqk.shape[0], sqk.shape[1]
        pack = PACK if key_heads % PACK == 0 else 1
        packs = key_heads // pack
        items = slots * spans * packs

    def forward(i):
        return pltpu.make_async_remote_copy(
            src_ref=outbox.at[i], dst_ref=inbox.at[i], send_sem=fsend.at[i],
            recv_sem=frecv.at[i], device_id={"seq": rank + 1}, device_id_type=pl.DeviceIdType.MESH,
        )

    def block(p, i):
        return finals.at[p, pl.ds(i * rep, rep)]

    def backward(i):
        return pltpu.make_async_remote_copy(
            src_ref=block(mine, i), dst_ref=block(mine, i), send_sem=bsend.at[i],
            recv_sem=brecv.at[i], device_id={"seq": rank - 1}, device_id_type=pl.DeviceIdType.MESH,
        )

    def across(p, i):
        return pltpu.make_async_remote_copy(
            src_ref=block(p, i), dst_ref=block(p, i), send_sem=csend.at[i],
            recv_sem=crecv.at[i], device_id={"prompt": other}, device_id_type=pl.DeviceIdType.MESH,
        )

    barrier = pltpu.get_barrier_semaphore()

    def greet(where):
        pl.semaphore_signal(barrier, inc=1, device_id=where, device_id_type=pl.DeviceIdType.MESH)

    greet({"prompt": other})

    @pl.when(rank > 0)
    def _():
        greet({"seq": rank - 1})

    @pl.when(rank < last)
    def _():
        greet({"seq": rank + 1})

    pl.semaphore_wait(
        barrier, 1 + jnp.where(rank > 0, 1, 0) + jnp.where(rank < last, 1, 0)
    )

    @pl.when(rank == 0)
    def _():
        inbox[...] = jnp.zeros_like(inbox)

    if work is not None:
        for s in range(slots):
            for c in range(spans):
                span = slice(c * CH, (c + 1) * CH)
                log_row = running_log(sdecay[s, :, span])
                beta_row = sbeta[s, :, span]
                log_col, beta_col = log_row.T, beta_row.T
                for j in range(key_heads):
                    scols[s, c, j] = gate_columns(log_col, beta_col, j, rep)
                    srows[s, c, j] = gate_rows(log_row, beta_row, j, rep)

    def step_forward(i):
        @pl.when(rank > 0)
        def _():
            forward(i).wait_recv()

        at = pl.ds(pl.multiple_of(i * rep * DV, rep * DV), rep * DV)
        v = pv[0, :, at]
        cols = pcols[0, 0, i]
        outs, grown = advance(
            rep,
            [
                (
                    pqk[0, 0, i],
                    [v[:, r * DV : (r + 1) * DV] for r in range(rep)],
                    [psolve[0, 0, i * rep + r] for r in range(rep)],
                    [pgram[0, 0, i * rep + r] for r in range(rep)],
                    cols,
                    [inbox[i, r] for r in range(rep)],
                )
            ],
        )

        @pl.when(rank < last)
        def _():
            for r in range(rep):
                outbox[i, r] = grown[r]
            forward(i).start()

        @pl.when(rank == last)
        def _():
            for r in range(rep):
                finals[mine, i * rep + r] = grown[r]

        pout[0, :, at] = jnp.concatenate(
            [norm_rows(o, gain).astype(BF16) for o in outs], axis=1
        )

    def step_back(i):
        @pl.when(rank < last)
        def _():
            backward(i).wait_recv()

        @pl.when(rank > 0)
        def _():
            backward(i).start()

        across(mine, i).start()

    def step_work(m):
        place, g = m // packs, m % packs
        s, c = place // spans, place % spans
        rows = pl.ds(pl.multiple_of(c * CH, CH), CH)
        at = pl.ds(pl.multiple_of(g * pack * DK, pack * DK), pack * DK)
        q, k = sq[s, rows, at], sk[s, rows, at]
        pairs, weights, solves = solve_spans(
            rep,
            [q[:, j * DK : (j + 1) * DK] for j in range(pack)],
            [k[:, j * DK : (j + 1) * DK] for j in range(pack)],
            [srows[s, c, g * pack + j] for j in range(pack)],
            [scols[s, c, g * pack + j] for j in range(pack)],
        )
        for j in range(pack):
            sqk[s, c, g * pack + j] = pairs[j]
        for h in range(pack * rep):
            sgram[s, c, g * pack * rep + h] = weights[h]
            ssolve[s, c, g * pack * rep + h] = solves[h]

    first_at = LAG * rank
    back_at = LAG * last + BACK * (last - rank)

    def tick(t, carry):
        i = t - first_at
        pl.when((i >= 0) & (i < key_heads))(lambda: step_forward(i))
        j = t - back_at
        pl.when((j >= 0) & (j < key_heads))(lambda: step_back(j))
        if work is not None:
            pl.when(t < items)(lambda: step_work(t))
        return carry

    lax.fori_loop(0, max(items, (LAG + BACK) * last + key_heads), tick, 0)

    def finish(i, carry):
        @pl.when(rank < last)
        def _():
            forward(i).wait_send()

        @pl.when(rank > 0)
        def _():
            backward(i).wait_send()

        across(mine, i).wait_send()
        across(other, i).wait_recv()
        return carry

    lax.fori_loop(0, key_heads, finish, 0)


LAG = 1
BACK = 2
PACK = 2
HALF_FROM = 16
OVERLAP = True


def group_of(key_heads):
    return 4 if key_heads % 4 == 0 else key_heads


PARAMS = dict(vmem_limit_bytes=60 * 1024 * 1024)


def prepare(q, k, beta, decay):
    slots, tokens, width = q.shape
    key_heads, heads = width // DK, beta.shape[1]
    rep, g, spans = heads // key_heads, group_of(width // DK), tokens // CH
    gate = pl.BlockSpec((1, g * rep, CH), lambda s, c, j: (s, j, c))
    rows = pl.BlockSpec((1, CH, g * DK), lambda s, c, j: (s, c, j))
    square = pl.BlockSpec((1, 1, g * rep, CH, CH), lambda s, c, j: (s, c, j, 0, 0))
    return pl.pallas_call(
        functools.partial(pre_kernel, rep),
        grid=(slots, spans, key_heads // g),
        in_specs=[rows, rows, gate, gate],
        out_specs=[
            pl.BlockSpec((1, 1, g, 2 * CH, DK), lambda s, c, j: (s, c, j, 0, 0)),
            square,
            square,
            pl.BlockSpec((1, 1, g, CH, 2 * rep), lambda s, c, j: (s, c, j, 0, 0)),
        ],
        out_shape=[
            jax.ShapeDtypeStruct((slots, spans, key_heads, 2 * CH, DK), BF16),
            jax.ShapeDtypeStruct((slots, spans, heads, CH, CH), BF16),
            jax.ShapeDtypeStruct((slots, spans, heads, CH, CH), BF16),
            jax.ShapeDtypeStruct((slots, spans, key_heads, CH, 2 * rep), F32),
        ],
        compiler_params=pltpu.CompilerParams(**PARAMS),
        cost_estimate=pl.CostEstimate(
            flops=slots * tokens * heads * CH * CH * 30, bytes_accessed=slots * tokens * heads * 800,
            transcendentals=slots * tokens * heads * CH,
        ),
        name="prepare",
    )(q, k, beta, decay)


def relay(terms, v, gain, suffix):
    key_heads, heads = terms[0].shape[2], terms[1].shape[2]
    rep = heads // key_heads
    count = lax.axis_size("prompt")
    vmem = pl.BlockSpec(memory_space=pltpu.VMEM)
    outs = [
        jax.ShapeDtypeStruct(v.shape, BF16),
        jax.ShapeDtypeStruct((count, heads, DK, DV), F32),
    ]
    scratch = [
        pltpu.VMEM((key_heads, rep, DK, DV), F32),
        pltpu.VMEM((key_heads, rep, DK, DV), F32),
    ] + [pltpu.SemaphoreType.DMA((key_heads,))] * 6
    args = [terms[0], v, terms[1], terms[2], terms[3], gain]
    body = functools.partial(relay_kernel, rep)
    if suffix is not None:
        q, k, beta, decay = suffix
        slots, spans = q.shape[0], q.shape[1] // CH
        work_outs = [
            jax.ShapeDtypeStruct((slots, spans, key_heads, 2 * CH, DK), BF16),
            jax.ShapeDtypeStruct((slots, spans, heads, CH, CH), BF16),
            jax.ShapeDtypeStruct((slots, spans, heads, CH, CH), BF16),
            jax.ShapeDtypeStruct((slots, spans, key_heads, CH, 2 * rep), F32),
        ]
        args += list(suffix)
        outs = outs + work_outs
        scratch = scratch[:2] + [pltpu.VMEM((slots, spans, key_heads, 2 * rep, CH), F32)] + scratch[2:]
    return pl.pallas_call(
        body,
        out_shape=outs,
        in_specs=[vmem] * len(args),
        out_specs=[vmem] * len(outs),
        scratch_shapes=scratch,
        compiler_params=pltpu.CompilerParams(
            collective_id=0, has_side_effects=True, vmem_limit_bytes=56 * 1024 * 1024
        ),
        name="relay",
    )(*args)


def sweep(terms, v, seeds, owner, length, gain):
    qk, solve, gram, cols = terms
    slots, spans, key_heads = qk.shape[:3]
    heads = solve.shape[2]
    rep, g, tokens = heads // key_heads, group_of(key_heads), spans * CH
    vals = pl.BlockSpec((1, tokens, g * rep * DV), lambda s, j, *_: (s, 0, j))
    square = pl.BlockSpec((1, spans, g * rep, CH, CH), lambda s, j, *_: (s, 0, j, 0, 0))
    return pl.pallas_call(
        functools.partial(seq_kernel, rep),
        grid_spec=pltpu.PrefetchScalarGridSpec(
            num_scalar_prefetch=2,
            grid=(slots, key_heads // g),
            in_specs=[
                pl.BlockSpec((1, spans, g, 2 * CH, DK), lambda s, j, *_: (s, 0, j, 0, 0)),
                vals,
                square,
                square,
                pl.BlockSpec((1, spans, g, CH, 2 * rep), lambda s, j, *_: (s, 0, j, 0, 0)),
                pl.BlockSpec((1, g * rep, DK, DV), lambda s, j, own, _: (own[s], j, 0, 0)),
                pl.BlockSpec((1, DV), lambda s, j, *_: (0, 0)),
            ],
            out_specs=vals,
        ),
        out_shape=jax.ShapeDtypeStruct(v.shape, BF16),
        compiler_params=pltpu.CompilerParams(**PARAMS),
        name="sweep",
    )(owner, length, qk, v, solve, gram, cols, seeds, gain)


def slot_facts(slot_branch, branch_length, branch_prompt, slot_count):
    rank = lax.axis_index("seq") * lax.axis_size("prompt") + lax.axis_index("prompt")
    slot_ids = rank * slot_count + jnp.arange(slot_count, dtype=jnp.int32)
    branch_ids = jnp.arange(slot_branch.shape[0], dtype=jnp.int32)
    mine = jnp.sum(
        jnp.where(slot_ids[:, None] == branch_ids[None, :], slot_branch[None, :], 0), axis=1
    )
    hit = mine[:, None] == branch_ids[None, :]
    length = jnp.sum(jnp.where(hit, branch_length[None, :], 0), axis=1)
    owner = jnp.sum(jnp.where(hit, branch_prompt[None, :], 0), axis=1)
    return length, owner


def local(
    prompt_queries, prompt_keys, prompt_values, prompt_beta, prompt_decay,
    suffix_queries, suffix_keys, suffix_values, suffix_beta, suffix_decay,
    norm_gain, slot_branch, branch_length, branch_prompt,
):
    gain = norm_gain[None, :]
    length, owner = slot_facts(slot_branch, branch_length, branch_prompt, suffix_queries.shape[0])
    terms = prepare(prompt_queries, prompt_keys, prompt_beta, prompt_decay)
    if OVERLAP:
        suffix = (suffix_queries, suffix_keys, suffix_beta, suffix_decay)
        prompt_out, finals, *suffix_terms = relay(terms, prompt_values, gain, suffix)
    else:
        prompt_out, finals = relay(terms, prompt_values, gain, None)
        suffix_terms = prepare(suffix_queries, suffix_keys, suffix_beta, suffix_decay)
    suffix_out = sweep(suffix_terms, suffix_values, finals, owner, length, gain)
    return (prompt_out, suffix_out)


def solution(mesh):
    lead = P(("groups", "prompt"), "seq", "head")
    lead_gate = P(("groups", "prompt"), "head", "seq")
    slot = P(("groups", "seq", "prompt"), None, "head")
    slot_gate = P(("groups", "seq", "prompt"), "head", None)
    return jax.shard_map(
        local,
        mesh=mesh,
        in_specs=(
            lead, lead, lead, lead_gate, lead_gate, slot, slot, slot, slot_gate, slot_gate,
            P(), P("groups"), P("groups"), P("groups"),
        ),
        out_specs=(lead, slot),
        check_vma=False,
    )
```

```python
import functools

import jax
import jax.numpy as jnp
from jax import lax
from jax.experimental import pallas as pl
from jax.experimental.pallas import tpu as pltpu
from jax.sharding import PartitionSpec as P

DK = 128
DV = 128
CH = 128
EPS_NORM = 1e-06
F32 = jnp.float32
BF16 = jnp.bfloat16
NN = (((1,), (0,)), ((), ()))
NT = (((1,), (1,)), ((), ()))
TN = (((0,), (0,)), ((), ()))


def mm(a, b, dims=NN):
    return lax.dot_general(a, b, dims, preferred_element_type=F32)


def unit(x):
    w = x.astype(F32)
    return (w * lax.rsqrt(jnp.sum(w * w, axis=-1, keepdims=True) + EPS_NORM)).astype(BF16)


def iotas():
    return (
        lax.broadcasted_iota(jnp.int32, (CH, CH), 0),
        lax.broadcasted_iota(jnp.int32, (CH, CH), 1),
    )


def running_log(decay):
    rows, cols = iotas()
    tri = jnp.where(rows <= cols, 1.0, 0.0).astype(F32)
    return lax.dot_general(
        decay, tri, NN, precision=lax.Precision.HIGHEST, preferred_element_type=F32
    )


def gate_columns(log_col, beta_col, j, rep):
    hs = slice(j * rep, (j + 1) * rep)
    return jnp.concatenate([log_col[:, hs], beta_col[:, hs]], axis=1)


def gate_rows(log_row, beta_row, j, rep):
    hs = slice(j * rep, (j + 1) * rep)
    return jnp.concatenate([log_row[hs], beta_row[hs]], axis=0)


def solve_spans(rep, queries, keys, gates_row, gates_col):
    rows, cols = iotas()
    upto = rows >= cols
    strict = rows > cols
    apart = rows ^ cols
    pairs, weights, lower = [], [], []
    for q, k, row, col in zip(queries, keys, gates_row, gates_col):
        q, k = unit(q), unit(k)
        pair = jnp.concatenate([q, k], axis=0)
        pairs.append(pair)
        grams = mm(pair, k, NT)
        for r in range(rep):
            spread = col[:, r : r + 1] - row[r : r + 1, :]
            ratio = jnp.exp(jnp.where(upto, spread, -1e30))
            weights.append((grams[:CH] * ratio).astype(BF16))
            beta = col[:, rep + r : rep + r + 1]
            lower.append(jnp.where(strict, beta * ratio * grams[CH:], 0.0))
    eye = jnp.where(rows == cols, 1.0, 0.0).astype(F32)
    first = strict & (apart == 1)
    inv = [eye - jnp.where(first, low, 0.0) for low in lower]
    level = 1
    while (1 << level) < CH:
        size = 1 << level
        pick = strict & ((apart >> level) == 1)
        inv16 = [t.astype(BF16) for t in inv]
        if size < HALF_FROM:
            mid = [mm(jnp.where(pick, low, 0.0).astype(BF16), t) for low, t in zip(lower, inv16)]
            inv = [t - mm(t16, x.astype(BF16)) for t, t16, x in zip(inv, inv16, mid)]
        else:
            starts = range(0, CH, 2 * size)

            def odd(x):
                return jnp.concatenate([x[i + size : i + 2 * size] for i in starts], axis=0)

            def spread_odd(x, fill):
                parts = []
                for n, i in enumerate(starts):
                    parts += [fill[i : i + size], x[n * size : (n + 1) * size]]
                return jnp.concatenate(parts, axis=0)

            blank = jnp.zeros((CH, CH), BF16)
            chosen = odd(pick.astype(F32)) > 0
            mid = [
                mm(jnp.where(chosen, odd(low), 0.0).astype(BF16), t)
                for low, t in zip(lower, inv16)
            ]
            inv = [
                spread_odd(odd(t) - mm(odd(t16), spread_odd(x.astype(BF16), blank)), t)
                for t, t16, x in zip(inv, inv16, mid)
            ]
        level += 1
    solves = []
    for h, t in enumerate(inv):
        row = gates_row[h // rep]
        r = rep + h % rep
        solves.append((jnp.where(strict, t, 0.0) * row[r : r + 1, :]).astype(BF16))
    return pairs, weights, solves


def pre_kernel(rep, q_ref, k_ref, beta_ref, decay_ref, qk_ref, solve_ref, gram_ref, cols_ref):
    key_heads = q_ref.shape[2] // DK
    log_row = running_log(decay_ref[0])
    log_col = log_row.T
    beta_row = beta_ref[0]
    beta_col = beta_row.T
    span = range(key_heads)
    cols = [gate_columns(log_col, beta_col, j, rep) for j in span]
    pairs, weights, solves = solve_spans(
        rep,
        [q_ref[0, :, j * DK : (j + 1) * DK] for j in span],
        [k_ref[0, :, j * DK : (j + 1) * DK] for j in span],
        [gate_rows(log_row, beta_row, j, rep) for j in span],
        cols,
    )
    for j in span:
        qk_ref[0, 0, j] = pairs[j]
        cols_ref[0, 0, j] = cols[j]
    for h in range(key_heads * rep):
        gram_ref[0, 0, h] = weights[h]
        solve_ref[0, 0, h] = solves[h]


def advance(rep, entries):
    heads = [(n, r) for n in range(len(entries)) for r in range(rep)]
    reads = [
        mm(e[0], jnp.concatenate([s.astype(BF16) for s in e[5]], axis=1)) for e in entries
    ]
    fades = [jnp.exp(entries[n][4][:, r : r + 1]) for n, r in heads]
    parts = [reads[n][:, r * DV : (r + 1) * DV] for n, r in heads]
    resids = [
        entries[n][1][r].astype(F32) - fade * part[CH:]
        for (n, r), fade, part in zip(heads, fades, parts)
    ]
    news = [
        entries[n][4][:, rep + r : rep + r + 1] * resid
        + mm(entries[n][2][r], resid.astype(BF16))
        for (n, r), resid in zip(heads, resids)
    ]
    ends = [entries[n][4][CH - 1 :, r : r + 1] for n, r in heads]
    tails = [
        (jnp.exp(end - entries[n][4][:, r : r + 1]) * new).astype(BF16)
        for (n, r), end, new in zip(heads, ends, news)
    ]
    grown = [
        mm(e[0][CH:], jnp.concatenate(tails[n * rep : (n + 1) * rep], axis=1), TN)
        for n, e in enumerate(entries)
    ]
    states = [
        jnp.exp(end) * entries[n][5][r] + grown[n][:, r * DV : (r + 1) * DV]
        for (n, r), end in zip(heads, ends)
    ]
    outs = [
        fade * part[:CH] + mm(entries[n][3][r], new.astype(BF16))
        for (n, r), fade, part, new in zip(heads, fades, parts, news)
    ]
    return outs, states


def norm_rows(o, gain):
    return o * lax.rsqrt(jnp.mean(o * o, axis=-1, keepdims=True) + EPS_NORM) * gain


def seq_kernel(
    rep, owner_ref, length_ref, qk_ref, v_ref, solve_ref, gram_ref, cols_ref, seed_ref,
    gain_ref, out_ref
):
    spans, key_heads = qk_ref.shape[1], qk_ref.shape[2]
    heads = key_heads * rep
    length = length_ref[pl.program_id(0)]
    gain = gain_ref[...]
    states = [seed_ref[0, h] for h in range(heads)]
    place = lax.broadcasted_iota(jnp.int32, (CH, DV), 0)
    for c in range(spans):
        span = slice(c * CH, (c + 1) * CH)
        live = place + c * CH < length
        outs, states = advance(
            rep,
            [
                (
                    qk_ref[0, c, j],
                    [v_ref[0, span, h * DV : (h + 1) * DV] for h in range(j * rep, (j + 1) * rep)],
                    [solve_ref[0, c, h] for h in range(j * rep, (j + 1) * rep)],
                    [gram_ref[0, c, h] for h in range(j * rep, (j + 1) * rep)],
                    cols_ref[0, c, j],
                    states[j * rep : (j + 1) * rep],
                )
                for j in range(key_heads)
            ],
        )
        for h, o in enumerate(outs):
            out_ref[0, span, h * DV : (h + 1) * DV] = jnp.where(
                live, norm_rows(o, gain), 0.0
            ).astype(BF16)


def relay_kernel(
    rep, pqk, pv, psolve, pgram, pcols, gain_ref, *rest
):
    if len(rest) == 10:
        work, rest = None, rest
    else:
        work, rest = rest[:4] + rest[6:10] + rest[12:13], rest[4:6] + rest[10:12] + rest[13:]
    pout, finals, inbox, outbox, fsend, frecv, bsend, brecv, csend, crecv = rest
    key_heads = pqk.shape[2]
    rank, last = lax.axis_index("seq"), lax.axis_size("seq") - 1
    mine = lax.axis_index("prompt")
    other = 1 - mine
    gain = gain_ref[...]
    items = 0
    if work is not None:
        sq, sk, sbeta, sdecay, sqk, ssolve, sgram, scols, srows = work
        slots, spans = sqk.shape[0], sqk.shape[1]
        pack = PACK if key_heads % PACK == 0 else 1
        packs = key_heads // pack
        items = slots * spans * packs

    def forward(i):
        return pltpu.make_async_remote_copy(
            src_ref=outbox.at[i], dst_ref=inbox.at[i], send_sem=fsend.at[i],
            recv_sem=frecv.at[i], device_id={"seq": rank + 1}, device_id_type=pl.DeviceIdType.MESH,
        )

    def block(p, i):
        return finals.at[p, pl.ds(i * rep, rep)]

    def backward(i):
        return pltpu.make_async_remote_copy(
            src_ref=block(mine, i), dst_ref=block(mine, i), send_sem=bsend.at[i],
            recv_sem=brecv.at[i], device_id={"seq": rank - 1}, device_id_type=pl.DeviceIdType.MESH,
        )

    def across(p, i):
        return pltpu.make_async_remote_copy(
            src_ref=block(p, i), dst_ref=block(p, i), send_sem=csend.at[i],
            recv_sem=crecv.at[i], device_id={"prompt": other}, device_id_type=pl.DeviceIdType.MESH,
        )

    barrier = pltpu.get_barrier_semaphore()

    def greet(where):
        pl.semaphore_signal(barrier, inc=1, device_id=where, device_id_type=pl.DeviceIdType.MESH)

    greet({"prompt": other})

    @pl.when(rank > 0)
    def _():
        greet({"seq": rank - 1})

    @pl.when(rank < last)
    def _():
        greet({"seq": rank + 1})

    pl.semaphore_wait(
        barrier, 1 + jnp.where(rank > 0, 1, 0) + jnp.where(rank < last, 1, 0)
    )

    @pl.when(rank == 0)
    def _():
        inbox[...] = jnp.zeros_like(inbox)

    def fill_gates():
        for s in range(slots):
            for c in range(spans):
                span = slice(c * CH, (c + 1) * CH)
                log_row = running_log(sdecay[s, :, span])
                beta_row = sbeta[s, :, span]
                log_col, beta_col = log_row.T, beta_row.T
                for j in range(key_heads):
                    scols[s, c, j] = gate_columns(log_col, beta_col, j, rep)
                    srows[s, c, j] = gate_rows(log_row, beta_row, j, rep)

    def step_forward(i):
        @pl.when(rank > 0)
        def _():
            forward(i).wait_recv()

        at = pl.ds(pl.multiple_of(i * rep * DV, rep * DV), rep * DV)
        v = pv[0, :, at]
        cols = pcols[0, 0, i]
        outs, grown = advance(
            rep,
            [
                (
                    pqk[0, 0, i],
                    [v[:, r * DV : (r + 1) * DV] for r in range(rep)],
                    [psolve[0, 0, i * rep + r] for r in range(rep)],
                    [pgram[0, 0, i * rep + r] for r in range(rep)],
                    cols,
                    [inbox[i, r] for r in range(rep)],
                )
            ],
        )

        @pl.when(rank < last)
        def _():
            for r in range(rep):
                outbox[i, r] = grown[r]
            forward(i).start()

        @pl.when(rank == last)
        def _():
            for r in range(rep):
                finals[mine, i * rep + r] = grown[r]

        pout[0, :, at] = jnp.concatenate(
            [norm_rows(o, gain).astype(BF16) for o in outs], axis=1
        )

    def step_back(i):
        @pl.when(rank < last)
        def _():
            backward(i).wait_recv()

        @pl.when(rank > 0)
        def _():
            backward(i).start()

        across(mine, i).start()

    def step_work(m):
        place, g = m // packs, m % packs
        s, c = place // spans, place % spans
        rows = pl.ds(pl.multiple_of(c * CH, CH), CH)
        at = pl.ds(pl.multiple_of(g * pack * DK, pack * DK), pack * DK)
        q, k = sq[s, rows, at], sk[s, rows, at]
        pairs, weights, solves = solve_spans(
            rep,
            [q[:, j * DK : (j + 1) * DK] for j in range(pack)],
            [k[:, j * DK : (j + 1) * DK] for j in range(pack)],
            [srows[s, c, g * pack + j] for j in range(pack)],
            [scols[s, c, g * pack + j] for j in range(pack)],
        )
        for j in range(pack):
            sqk[s, c, g * pack + j] = pairs[j]
        for h in range(pack * rep):
            sgram[s, c, g * pack * rep + h] = weights[h]
            ssolve[s, c, g * pack * rep + h] = solves[h]

    first_at = LAG * rank
    back_at = LAG * last + BACK * (last - rank)

    def tick(t, carry):
        i = t - first_at
        pl.when((i >= 0) & (i < key_heads))(lambda: step_forward(i))
        if work is not None:
            pl.when(t == 0)(fill_gates)
        j = t - back_at
        pl.when((j >= 0) & (j < key_heads))(lambda: step_back(j))
        if work is not None:
            pl.when(t < items)(lambda: step_work(t))
        return carry

    lax.fori_loop(0, max(items, (LAG + BACK) * last + key_heads), tick, 0)

    def finish(i, carry):
        @pl.when(rank < last)
        def _():
            forward(i).wait_send()

        @pl.when(rank > 0)
        def _():
            backward(i).wait_send()

        across(mine, i).wait_send()
        across(other, i).wait_recv()
        return carry

    lax.fori_loop(0, key_heads, finish, 0)


LAG = 1
BACK = 2
PACK = 4
HALF_FROM = 16
OVERLAP = True


def group_of(key_heads):
    return 4 if key_heads % 4 == 0 else key_heads


PARAMS = dict(vmem_limit_bytes=60 * 1024 * 1024)


def prepare(q, k, beta, decay):
    slots, tokens, width = q.shape
    key_heads, heads = width // DK, beta.shape[1]
    rep, g, spans = heads // key_heads, group_of(width // DK), tokens // CH
    gate = pl.BlockSpec((1, g * rep, CH), lambda s, c, j: (s, j, c))
    rows = pl.BlockSpec((1, CH, g * DK), lambda s, c, j: (s, c, j))
    square = pl.BlockSpec((1, 1, g * rep, CH, CH), lambda s, c, j: (s, c, j, 0, 0))
    return pl.pallas_call(
        functools.partial(pre_kernel, rep),
        grid=(slots, spans, key_heads // g),
        in_specs=[rows, rows, gate, gate],
        out_specs=[
            pl.BlockSpec((1, 1, g, 2 * CH, DK), lambda s, c, j: (s, c, j, 0, 0)),
            square,
            square,
            pl.BlockSpec((1, 1, g, CH, 2 * rep), lambda s, c, j: (s, c, j, 0, 0)),
        ],
        out_shape=[
            jax.ShapeDtypeStruct((slots, spans, key_heads, 2 * CH, DK), BF16),
            jax.ShapeDtypeStruct((slots, spans, heads, CH, CH), BF16),
            jax.ShapeDtypeStruct((slots, spans, heads, CH, CH), BF16),
            jax.ShapeDtypeStruct((slots, spans, key_heads, CH, 2 * rep), F32),
        ],
        compiler_params=pltpu.CompilerParams(**PARAMS),
        cost_estimate=pl.CostEstimate(
            flops=slots * tokens * heads * CH * CH * 30, bytes_accessed=slots * tokens * heads * 800,
            transcendentals=slots * tokens * heads * CH,
        ),
        name="prepare",
    )(q, k, beta, decay)


def relay(terms, v, gain, suffix):
    key_heads, heads = terms[0].shape[2], terms[1].shape[2]
    rep = heads // key_heads
    count = lax.axis_size("prompt")
    vmem = pl.BlockSpec(memory_space=pltpu.VMEM)
    outs = [
        jax.ShapeDtypeStruct(v.shape, BF16),
        jax.ShapeDtypeStruct((count, heads, DK, DV), F32),
    ]
    scratch = [
        pltpu.VMEM((key_heads, rep, DK, DV), F32),
        pltpu.VMEM((key_heads, rep, DK, DV), F32),
    ] + [pltpu.SemaphoreType.DMA((key_heads,))] * 6
    args = [terms[0], v, terms[1], terms[2], terms[3], gain]
    body = functools.partial(relay_kernel, rep)
    if suffix is not None:
        q, k, beta, decay = suffix
        slots, spans = q.shape[0], q.shape[1] // CH
        work_outs = [
            jax.ShapeDtypeStruct((slots, spans, key_heads, 2 * CH, DK), BF16),
            jax.ShapeDtypeStruct((slots, spans, heads, CH, CH), BF16),
            jax.ShapeDtypeStruct((slots, spans, heads, CH, CH), BF16),
            jax.ShapeDtypeStruct((slots, spans, key_heads, CH, 2 * rep), F32),
        ]
        args += list(suffix)
        outs = outs + work_outs
        scratch = scratch[:2] + [pltpu.VMEM((slots, spans, key_heads, 2 * rep, CH), F32)] + scratch[2:]
    return pl.pallas_call(
        body,
        out_shape=outs,
        in_specs=[vmem] * len(args),
        out_specs=[vmem] * len(outs),
        scratch_shapes=scratch,
        compiler_params=pltpu.CompilerParams(
            collective_id=0, has_side_effects=True, vmem_limit_bytes=56 * 1024 * 1024
        ),
        name="relay",
    )(*args)


def sweep(terms, v, seeds, owner, length, gain):
    qk, solve, gram, cols = terms
    slots, spans, key_heads = qk.shape[:3]
    heads = solve.shape[2]
    rep, g, tokens = heads // key_heads, group_of(key_heads), spans * CH
    vals = pl.BlockSpec((1, tokens, g * rep * DV), lambda s, j, *_: (s, 0, j))
    square = pl.BlockSpec((1, spans, g * rep, CH, CH), lambda s, j, *_: (s, 0, j, 0, 0))
    return pl.pallas_call(
        functools.partial(seq_kernel, rep),
        grid_spec=pltpu.PrefetchScalarGridSpec(
            num_scalar_prefetch=2,
            grid=(slots, key_heads // g),
            in_specs=[
                pl.BlockSpec((1, spans, g, 2 * CH, DK), lambda s, j, *_: (s, 0, j, 0, 0)),
                vals,
                square,
                square,
                pl.BlockSpec((1, spans, g, CH, 2 * rep), lambda s, j, *_: (s, 0, j, 0, 0)),
                pl.BlockSpec((1, g * rep, DK, DV), lambda s, j, own, _: (own[s], j, 0, 0)),
                pl.BlockSpec((1, DV), lambda s, j, *_: (0, 0)),
            ],
            out_specs=vals,
        ),
        out_shape=jax.ShapeDtypeStruct(v.shape, BF16),
        compiler_params=pltpu.CompilerParams(**PARAMS),
        name="sweep",
    )(owner, length, qk, v, solve, gram, cols, seeds, gain)


def slot_facts(slot_branch, branch_length, branch_prompt, slot_count):
    rank = lax.axis_index("seq") * lax.axis_size("prompt") + lax.axis_index("prompt")
    slot_ids = rank * slot_count + jnp.arange(slot_count, dtype=jnp.int32)
    branch_ids = jnp.arange(slot_branch.shape[0], dtype=jnp.int32)
    mine = jnp.sum(
        jnp.where(slot_ids[:, None] == branch_ids[None, :], slot_branch[None, :], 0), axis=1
    )
    hit = mine[:, None] == branch_ids[None, :]
    length = jnp.sum(jnp.where(hit, branch_length[None, :], 0), axis=1)
    owner = jnp.sum(jnp.where(hit, branch_prompt[None, :], 0), axis=1)
    return length, owner


def local(
    prompt_queries, prompt_keys, prompt_values, prompt_beta, prompt_decay,
    suffix_queries, suffix_keys, suffix_values, suffix_beta, suffix_decay,
    norm_gain, slot_branch, branch_length, branch_prompt,
):
    gain = norm_gain[None, :]
    length, owner = slot_facts(slot_branch, branch_length, branch_prompt, suffix_queries.shape[0])
    terms = prepare(prompt_queries, prompt_keys, prompt_beta, prompt_decay)
    if OVERLAP:
        suffix = (suffix_queries, suffix_keys, suffix_beta, suffix_decay)
        prompt_out, finals, *suffix_terms = relay(terms, prompt_values, gain, suffix)
    else:
        prompt_out, finals = relay(terms, prompt_values, gain, None)
        suffix_terms = prepare(suffix_queries, suffix_keys, suffix_beta, suffix_decay)
    suffix_out = sweep(suffix_terms, suffix_values, finals, owner, length, gain)
    return (prompt_out, suffix_out)


def solution(mesh):
    lead = P(("groups", "prompt"), "seq", "head")
    lead_gate = P(("groups", "prompt"), "head", "seq")
    slot = P(("groups", "seq", "prompt"), None, "head")
    slot_gate = P(("groups", "seq", "prompt"), "head", None)
    return jax.shard_map(
        local,
        mesh=mesh,
        in_specs=(
            lead, lead, lead, lead_gate, lead_gate, slot, slot, slot, slot_gate, slot_gate,
            P(), P("groups"), P("groups"), P("groups"),
        ),
        out_specs=(lead, slot),
        check_vma=False,
    )
```
